1024 devices in a mesh: mp: 64 (over z, y), dp: 16 (over x, core).
Axes of the slice: x: 8, y: 8, z: 8, core: 2. Of those that a mesh axis runs over, the one named last changes fastest.
Arguments:
- momentum: float32 [8192, 28672], P('mp', 'dp'), may hold values from -120 to 120, as said below
- gradient: bfloat16 [8192, 28672], P('mp', 'dp'), may hold values from -4 to 4
- factor_q: bfloat16 [28672, 128], P(('dp', 'mp')), may hold values from -0.03125 to 0.03125
Outputs:
- momentum_out: float32 [8192, 28672], P('mp', 'dp')
- factor_out: bfloat16 [28672, 128], P(('dp', 'mp'))
- update: bfloat16 [8192, 28672], P('mp', 'dp')
The draws below stay inside these ranges and needn't reach their ends.
Inputs may be any that keep to these rules, and one draw needn't show every extreme that they name: `momentum`: entries are finite reals.
All inputs are finite; a program needn't handle non-finite values.
Results may differ from the reference program's by a relative error of at most 0.00135.
Values may be sent and summed in bfloat16 or wider, within the bound.
No kernel may reach another device: no remote copies, remote signals or barrier semaphores. Data moves between devices by JAX's collectives and lax.ppermute only.
A program may use at most 32 MiB of HBM per device.

```python
import math
import jax
import jax.numpy as jnp
from jax import lax

D = 8192
FF = 28672
RANK = 128


def draw_momentum(key, part):
    keys = jax.random.split(key, 6)
    row_ramp = 3.0 ** (jnp.arange(D, dtype=jnp.float32) / (D - 1))
    col_ramp = 3.0 ** (jnp.arange(FF, dtype=jnp.float32) / (FF - 1))
    row_scale = 0.5 * row_ramp * jnp.exp(jax.random.uniform(keys[0], (D,), jnp.float32, 0.0, math.log(10.0 / 3.0)))
    col_scale = 0.4 * col_ramp * jnp.exp(jax.random.uniform(keys[1], (FF,), jnp.float32, 0.0, math.log(10.0 / 3.0)))
    base = jax.random.normal(keys[5], (D, FF), jnp.float32)
    base = jnp.clip(base, -6.0, 6.0)
    return (base * row_scale[:, None] * col_scale[None, :]).astype(jnp.float32)


def levels(own_key, shape, cuts, smallest, top_value):
    loudness = 1.0
    for position, blocks in cuts:
        steps = jax.random.uniform(jax.random.fold_in(jax.random.fold_in(own_key, 6), position), (blocks,), jnp.float32, smallest / len(cuts), top_value / len(cuts))
        loudness = loudness * jnp.repeat(jnp.exp(steps), shape[position] // blocks).reshape((-1,) + (1,) * (len(shape) - 1 - position))
    return loudness


def noise(stream_key, extent, scale, limit, pieces=(), kind=jnp.bfloat16):
    gain = levels(stream_key, extent, pieces, -0.22, 0.18) if pieces else 1.0
    drawn = jax.random.normal(stream_key, extent, jnp.float32) * scale * gain
    return jnp.minimum(jnp.maximum(drawn, -limit), limit).astype(kind)


def setup_inputs(seed: int = 0) -> dict:
    splits = jax.random.split(jax.random.key(seed), 4)
    return {
        "momentum": draw_momentum(jax.random.fold_in(splits[3], 71), 0),
        "gradient": noise(splits[1], (D, FF), 0.5, 4.0, ((0, 64), (1, 16))),
        "factor_q": noise(splits[2], (FF, RANK), FF ** -0.5, 0.03125, ((0, 1024),)),
    }


highest = lax.Precision.HIGHEST
feedback_rate = 0.05

def reference(momentum, gradient, factor_q):
    blended = momentum + gradient.astype(jnp.float32)
    power_left = jnp.dot(blended, factor_q.astype(jnp.float32), precision=highest)
    gram_matrix = jnp.dot(power_left.T, power_left, precision=highest)
    factor_low = jnp.linalg.cholesky(gram_matrix)
    orthonormal = jax.scipy.linalg.solve_triangular(factor_low, power_left.T, lower=True).T
    power_right = jnp.dot(blended.T, orthonormal, precision=highest)
    column_sums = lax.optimization_barrier(jnp.sum(power_right * power_right, axis=0))
    q_new = power_right * lax.rsqrt(column_sums + 1e-06)
    momentum_out = blended - feedback_rate * jnp.dot(orthonormal, power_right.T, precision=highest)
    scale_factor = math.sqrt(D * FF / RANK)
    update = (scale_factor * jnp.dot(orthonormal, q_new.T, precision=highest)).astype(jnp.bfloat16)
    return (momentum_out, q_new.astype(jnp.bfloat16), update)
```

```python
import math

import jax
import jax.numpy as jnp
from jax import lax
from jax.sharding import Mesh
from jax.sharding import PartitionSpec as P

D = 8192
FF = 28672
RANK = 128
SIDE = 8
SHARE = 28
SLOT = 32

highest = lax.Precision.HIGHEST
feedback_rate = 0.05


def exchange(blocks, axis):
    return lax.all_to_all(blocks, axis, 0, 0, tiled=False)


def gather_blocks(block, axis, size):
    return exchange(jnp.broadcast_to(block[None], (size, *block.shape)), axis)


def sum_over_dp(part):
    rows = part.shape[0] // 2
    core = lax.axis_index("c")
    kept = lax.dynamic_slice_in_dim(part, core * rows, rows, 0)
    given = lax.dynamic_slice_in_dim(part, (1 - core) * rows, rows, 0)
    half = kept + lax.ppermute(given, "c", [(0, 1), (1, 0)])
    piece = jnp.sum(exchange(half.reshape(SIDE, rows // SIDE, RANK), "x"), axis=0)
    half = gather_blocks(piece, "x", SIDE).reshape(rows, RANK)
    other = lax.ppermute(half, "c", [(0, 1), (1, 0)])
    low = jnp.where(core == 0, half, other)
    high = jnp.where(core == 0, other, half)
    return jnp.concatenate([low, high], axis=0)


def local(momentum, gradient, factor_q):
    blended = momentum + gradient.astype(jnp.float32)
    cols_local = blended.shape[1]
    q_cols = gather_blocks(factor_q, ("z", "y"), SIDE * SIDE).reshape(cols_local, RANK)
    power_left = sum_over_dp(jnp.dot(blended, q_cols.astype(jnp.float32), precision=highest))
    gram_part = jnp.dot(power_left.T, power_left, precision=highest)
    raw_part = jnp.dot(blended.T, power_left, precision=highest)
    payload = jnp.concatenate(
        [
            raw_part.reshape(SIDE, SIDE, SHARE, RANK),
            gram_part.reshape(SIDE, SIDE, 2, RANK),
            jnp.zeros((SIDE, SIDE, SLOT - SHARE - 2, RANK), jnp.float32),
        ],
        axis=2,
    )
    over_z = jnp.sum(exchange(payload, "z"), axis=0)
    slot = jnp.sum(exchange(over_z, "y"), axis=0)
    slots = gather_blocks(gather_blocks(slot, "y", SIDE), "z", SIDE)
    gram_matrix = slots[:, :, SHARE : SHARE + 2].reshape(RANK, RANK)
    raw = slots[:, :, :SHARE].reshape(cols_local, RANK)
    factor_low = jnp.linalg.cholesky(gram_matrix)
    inverse_low = jax.scipy.linalg.solve_triangular(factor_low, jnp.eye(RANK, dtype=jnp.float32), lower=True)
    orthonormal = jnp.dot(power_left, inverse_low.T, precision=highest)
    power_right = jnp.dot(raw, inverse_low.T, precision=highest)
    sums = jnp.sum(power_right * power_right, axis=0, keepdims=True)
    sums = sums + lax.ppermute(sums, "c", [(0, 1), (1, 0)])
    column_sums = jnp.sum(gather_blocks(sums, "x", SIDE), axis=(0, 1))
    norm = lax.rsqrt(column_sums + 1e-06)
    share = jnp.dot(slot[:SHARE], inverse_low.T, precision=highest)
    momentum_out = blended - feedback_rate * jnp.dot(orthonormal, power_right.T, precision=highest)
    scale_factor = math.sqrt(D * FF / RANK)
    update = jnp.dot(orthonormal * (norm * scale_factor), power_right.T, precision=highest).astype(jnp.bfloat16)
    return (momentum_out, (share * norm).astype(jnp.bfloat16), update)


def solution(mesh):
    grid = Mesh(mesh.devices.reshape(SIDE, SIDE, SIDE, 2), ("z", "y", "x", "c"))
    mp, dp = ("z", "y"), ("x", "c")
    return jax.shard_map(
        local,
        mesh=grid,
        in_specs=(P(mp, dp), P(mp, dp), P((*dp, *mp), None)),
        out_specs=(P(mp, dp), P((*dp, *mp), None), P(mp, dp)),
        check_vma=False,
    )
```

```python
import math

import jax
import jax.numpy as jnp
from jax import lax
from jax.experimental import pallas as pl
from jax.experimental.pallas import tpu as pltpu
from jax.sharding import Mesh
from jax.sharding import PartitionSpec as P

D = 8192
FF = 28672
RANK = 128
SIDE = 8
SHARE = 28
PANEL = 16

highest = lax.Precision.HIGHEST
feedback_rate = 0.05


def invert_low(gram_ref, out_ref, work_ref):
    rows = lax.broadcasted_iota(jnp.int32, (RANK, RANK), 0)
    lanes = lax.broadcasted_iota(jnp.int32, (RANK, RANK), 1)
    work_ref[:, :RANK] = gram_ref[...]
    work_ref[:, RANK:] = jnp.where(rows == lanes, 1.0, 0.0).astype(jnp.float32)
    own = lax.broadcasted_iota(jnp.int32, (PANEL, RANK), 0)
    for first in range(0, RANK, PANEL):
        last = first + PANEL
        panel = work_ref[first:last, :RANK]
        extra = work_ref[first:last, RANK:]
        cols = [jnp.broadcast_to(panel[:, first + t : first + t + 1], (PANEL, RANK)) for t in range(PANEL)]
        pivots = jnp.ones((PANEL, RANK), jnp.float32)
        for t in range(PANEL):
            pivot = jnp.broadcast_to(cols[t][t : t + 1], (PANEL, RANK))
            pivots = jnp.where(own == t, pivot, pivots)
            if t + 1 < PANEL:
                factor = jnp.where(own > t, cols[t] / pivot, 0.0)
                panel = panel - factor * panel[t : t + 1]
                extra = extra - factor * extra[t : t + 1]
                for u in range(t + 1, PANEL):
                    cols[u] = cols[u] - factor * cols[u][t : t + 1]
        out_ref[first:last] = extra * lax.rsqrt(pivots)
        if last < RANK:
            both = jnp.concatenate([panel, extra], axis=1)
            taken = lax.dot_general(
                panel / pivots,
                both,
                (((0,), (0,)), ((), ())),
                precision=highest,
                preferred_element_type=jnp.float32,
            )
            work_ref[last:] = work_ref[last:] - taken[last:]


def inverse_cholesky(gram_matrix):
    return pl.pallas_call(
        invert_low,
        out_shape=jax.ShapeDtypeStruct((RANK, RANK), jnp.float32),
        scratch_shapes=[pltpu.VMEM((RANK, 2 * RANK), jnp.float32)],
        name="invert_low",
    )(gram_matrix)


def exchange(blocks, axis):
    return lax.all_to_all(blocks, axis, 0, 0, tiled=False)


def gather_blocks(block, axis, size):
    return exchange(jnp.broadcast_to(block[None], (size, *block.shape)), axis)


def sum_over_dp(part):
    rows = part.shape[0] // 2
    core = lax.axis_index("c")
    kept = lax.dynamic_slice_in_dim(part, core * rows, rows, 0)
    given = lax.dynamic_slice_in_dim(part, (1 - core) * rows, rows, 0)
    half = kept + lax.ppermute(given, "c", [(0, 1), (1, 0)])
    half = jnp.sum(gather_blocks(half, "x", SIDE), axis=0)
    other = lax.ppermute(half, "c", [(0, 1), (1, 0)])
    low = jnp.where(core == 0, half, other)
    high = jnp.where(core == 0, other, half)
    return jnp.concatenate([low, high], axis=0)


def local(momentum, gradient, factor_q):
    blended = momentum + gradient.astype(jnp.float32)
    cols_local = blended.shape[1]
    q_cols = gather_blocks(factor_q, ("z", "y"), SIDE * SIDE).reshape(cols_local, RANK)
    power_left = sum_over_dp(jnp.dot(blended, q_cols.astype(jnp.float32), precision=highest))
    gram_part = jnp.dot(power_left.T, power_left, precision=highest)
    raw_part = jnp.dot(blended.T, power_left, precision=highest)
    slots = jnp.concatenate([raw_part.reshape(SIDE * SIDE, SHARE, RANK), gram_part.reshape(SIDE * SIDE, 2, RANK)], axis=1)
    slot = jnp.sum(exchange(slots, ("z", "y")), axis=0)
    slots = gather_blocks(slot, ("z", "y"), SIDE * SIDE)
    gram_matrix = slots[:, SHARE:].reshape(RANK, RANK)
    raw = slots[:, :SHARE].reshape(cols_local, RANK)
    inverse_low = inverse_cholesky(gram_matrix)
    orthonormal = jnp.dot(power_left, inverse_low.T, precision=highest)
    power_right = jnp.dot(raw, inverse_low.T, precision=highest)
    sums = jnp.sum(power_right * power_right, axis=0, keepdims=True)
    column_sums = jnp.sum(gather_blocks(sums, ("x", "c"), 2 * SIDE), axis=(0, 1))
    norm = lax.rsqrt(column_sums + 1e-06)
    share = jnp.dot(slot[:SHARE], inverse_low.T, precision=highest)
    momentum_out = blended - feedback_rate * jnp.dot(orthonormal, power_right.T, precision=highest)
    scale_factor = math.sqrt(D * FF / RANK)
    update = jnp.dot(orthonormal * (norm * scale_factor), power_right.T, precision=highest).astype(jnp.bfloat16)
    return (momentum_out, (share * norm).astype(jnp.bfloat16), update)


def solution(mesh):
    grid = Mesh(mesh.devices.reshape(SIDE, SIDE, SIDE, 2), ("z", "y", "x", "c"))
    mp, dp = ("z", "y"), ("x", "c")
    return jax.shard_map(
        local,
        mesh=grid,
        in_specs=(P(mp, dp), P(mp, dp), P((*dp, *mp), None)),
        out_specs=(P(mp, dp), P((*dp, *mp), None), P(mp, dp)),
        check_vma=False,
    )
```

```python
import math

import jax
import jax.numpy as jnp
from jax import lax
from jax.experimental import pallas as pl
from jax.experimental.pallas import tpu as pltpu
from jax.sharding import Mesh
from jax.sharding import PartitionSpec as P

D = 8192
FF = 28672
RANK = 128
SIDE = 8
SHARE = 28
PANEL = 16
PART_SCALE = 2.0**-4
SUM_SCALE = 2.0**-7
GRAM_PART_SCALE = 2.0**-8
GRAM_SUM_SCALE = 2.0**-11
GRAM_FLOOR = 0.125
SPREAD = 1.25
HALF_NOISE = 4.4e-08
NOISE_FLOOR = FF // 16 * 3.0e-16 * (1 + 64 * (SUM_SCALE / PART_SCALE) ** 2)
NOISE_LIMIT = 1.6e-07

highest = lax.Precision.HIGHEST
feedback_rate = 0.05


def invert_low(gram_ref, out_ref, work_ref):
    rows = lax.broadcasted_iota(jnp.int32, (RANK, RANK), 0)
    lanes = lax.broadcasted_iota(jnp.int32, (RANK, RANK), 1)
    work_ref[:, :RANK] = gram_ref[...]
    work_ref[:, RANK:] = jnp.where(rows == lanes, 1.0, 0.0).astype(jnp.float32)
    own = lax.broadcasted_iota(jnp.int32, (PANEL, RANK), 0)
    for first in range(0, RANK, PANEL):
        last = first + PANEL
        panel = work_ref[first:last, :RANK]
        extra = work_ref[first:last, RANK:]
        cols = [jnp.broadcast_to(panel[:, first + t : first + t + 1], (PANEL, RANK)) for t in range(PANEL)]
        pivots = jnp.ones((PANEL, RANK), jnp.float32)
        for t in range(PANEL):
            pivot = jnp.broadcast_to(cols[t][t : t + 1], (PANEL, RANK))
            pivots = jnp.where(own == t, pivot, pivots)
            if t + 1 < PANEL:
                factor = jnp.where(own > t, cols[t] / pivot, 0.0)
                panel = panel - factor * panel[t : t + 1]
                extra = extra - factor * extra[t : t + 1]
                for u in range(t + 1, PANEL):
                    cols[u] = cols[u] - factor * cols[u][t : t + 1]
        out_ref[first:last] = extra * lax.rsqrt(pivots)
        if last < RANK:
            both = jnp.concatenate([panel, extra], axis=1)
            taken = lax.dot_general(
                panel / pivots,
                both,
                (((0,), (0,)), ((), ())),
                precision=highest,
                preferred_element_type=jnp.float32,
            )
            work_ref[last:] = work_ref[last:] - taken[last:]


def inverse_cholesky(gram_matrix):
    return pl.pallas_call(
        invert_low,
        out_shape=jax.ShapeDtypeStruct((RANK, RANK), jnp.float32),
        scratch_shapes=[pltpu.VMEM((RANK, 2 * RANK), jnp.float32)],
        name="invert_low",
    )(gram_matrix)


def exchange(blocks, axis):
    return lax.all_to_all(blocks, axis, 0, 0, tiled=False)


def gather_blocks(block, axis, size):
    return exchange(jnp.broadcast_to(block[None], (size, *block.shape)), axis)


def sum_over_dp(part):
    rows = part.shape[0] // 2
    core = lax.axis_index("c")
    kept = lax.dynamic_slice_in_dim(part, core * rows, rows, 0)
    given = lax.dynamic_slice_in_dim(part, (1 - core) * rows, rows, 0)
    half = kept + lax.ppermute(given, "c", [(0, 1), (1, 0)])
    half = jnp.sum(gather_blocks(half, "x", SIDE), axis=0)
    other = lax.ppermute(half, "c", [(0, 1), (1, 0)])
    low = jnp.where(core == 0, half, other)
    high = jnp.where(core == 0, other, half)
    return jnp.concatenate([low, high], axis=0)


def to_half(rows, gram_rows, row_scale, gram_scale):
    gram_rows = gram_rows * gram_scale
    high = lax.reduce_precision(gram_rows, 5, 10)
    low = (gram_rows - high) * 2048.0
    return jnp.concatenate([(v).astype(jnp.float16) for v in (rows * row_scale, high, low)], axis=1)


def gram_of(packed, gram_scale):
    high = packed[:, SHARE : SHARE + 2].astype(jnp.float32)
    low = packed[:, SHARE + 2 :].astype(jnp.float32)
    return (high + low * (1.0 / 2048.0)) * (1.0 / gram_scale)


def outputs(blended, orthonormal, power_right, share, norm):
    momentum_out = blended - feedback_rate * jnp.dot(orthonormal, power_right.T, precision=highest)
    scale_factor = math.sqrt(D * FF / RANK)
    update = jnp.dot(orthonormal * (norm * scale_factor), power_right.T, precision=highest).astype(jnp.bfloat16)
    return (momentum_out, (share * norm).astype(jnp.bfloat16), update)


def scales(column_sums):
    return lax.rsqrt(column_sums + 1e-06)


def full_precision(blended, power_left, raw_part, gram_part):
    count = SIDE * SIDE
    slots = jnp.concatenate([raw_part.reshape(count, SHARE, RANK), gram_part.reshape(count, 2, RANK)], axis=1)
    slot = jnp.sum(exchange(slots, ("z", "y")), axis=0)
    slots = gather_blocks(slot, ("z", "y"), count)
    inverse_low = inverse_cholesky(slots[:, SHARE:].reshape(RANK, RANK))
    orthonormal = jnp.dot(power_left, inverse_low.T, precision=highest)
    power_right = jnp.dot(slots[:, :SHARE].reshape(count * SHARE, RANK), inverse_low.T, precision=highest)
    sums = jnp.sum(power_right * power_right, axis=0, keepdims=True)
    norm = scales(jnp.sum(gather_blocks(sums, ("x", "c"), 2 * SIDE), axis=(0, 1)))
    share = jnp.dot(slot[:SHARE], inverse_low.T, precision=highest)
    return outputs(blended, orthonormal, power_right, share, norm)


def local(momentum, gradient, factor_q):
    blended = momentum + gradient.astype(jnp.float32)
    cols_local = blended.shape[1]
    count = SIDE * SIDE
    q_cols = gather_blocks(factor_q, ("z", "y"), count).reshape(cols_local, RANK)
    power_left = sum_over_dp(jnp.dot(blended, q_cols.astype(jnp.float32), precision=highest))
    gram_part = jnp.dot(power_left.T, power_left, precision=highest)
    raw_part = jnp.dot(blended.T, power_left, precision=highest)
    packed = to_half(raw_part.reshape(count, SHARE, RANK), gram_part.reshape(count, 2, RANK), PART_SCALE, GRAM_PART_SCALE)
    packed = exchange(packed, ("z", "y"))
    rows = packed[:, :SHARE].astype(jnp.float32)
    total = jnp.sum(rows, axis=0)
    cancelled = jnp.sum(rows * rows) > SPREAD * jnp.sum(total * total)
    slot = jnp.where(cancelled, jnp.inf, total * (1.0 / PART_SCALE))
    gram_slot = jnp.sum(gram_of(packed, GRAM_PART_SCALE), axis=0)
    packed = gather_blocks(to_half(slot[None], gram_slot[None], SUM_SCALE, GRAM_SUM_SCALE)[0], ("z", "y"), count)
    rows = lax.optimization_barrier(packed[:, :SHARE].reshape(cols_local, RANK)).astype(jnp.float32)
    gram_rows = gram_of(packed, GRAM_SUM_SCALE)
    gram_matrix = gram_rows.reshape(RANK, RANK)
    inverse_low = inverse_cholesky(gram_matrix)
    orthonormal = jnp.dot(power_left, inverse_low.T, precision=highest)
    power_right = jnp.dot(rows, inverse_low.T * (1.0 / SUM_SCALE), precision=highest)
    sums = jnp.sum(power_right * power_right, axis=0)
    noise = jnp.sum(rows * rows, axis=0) * (HALF_NOISE * (1.0 + SPREAD)) + NOISE_FLOOR
    noise = jnp.sum(inverse_low * inverse_low * noise, axis=1) * (1.0 / SUM_SCALE**2)
    both = jnp.sum(gather_blocks(jnp.stack([sums, noise]), ("x", "c"), 2 * SIDE), axis=0)
    norm = scales(both[0])
    diagonal = jnp.max(jnp.where(jnp.eye(RANK, dtype=bool), gram_matrix, 0.0), axis=1)
    fine = (jnp.mean(both[1] / both[0]) < NOISE_LIMIT) & (jnp.min(diagonal) > GRAM_FLOOR)
    share = jnp.dot(slot, inverse_low.T, precision=highest)
    return lax.cond(
        fine,
        lambda: outputs(blended, orthonormal, power_right, share, norm),
        lambda: full_precision(blended, power_left, raw_part, gram_part),
    )


def solution(mesh):
    grid = Mesh(mesh.devices.reshape(SIDE, SIDE, SIDE, 2), ("z", "y", "x", "c"))
    mp, dp = ("z", "y"), ("x", "c")
    return jax.shard_map(
        local,
        mesh=grid,
        in_specs=(P(mp, dp), P(mp, dp), P((*dp, *mp), None)),
        out_specs=(P(mp, dp), P((*dp, *mp), None), P(mp, dp)),
        check_vma=False,
    )
```

```python
import math

import jax
import jax.numpy as jnp
from jax import lax
from jax.experimental import pallas as pl
from jax.experimental.pallas import tpu as pltpu
from jax.sharding import Mesh
from jax.sharding import PartitionSpec as P

D = 8192
FF = 28672
RANK = 128
SIDE = 8
SHARE = 28
PANEL = 16
PART_SCALE = 2.0**-4
SUM_SCALE = 2.0**-7
GRAM_PART_SCALE = 2.0**-8
GRAM_SUM_SCALE = 2.0**-11
GRAM_FLOOR = 0.125
SPREAD = 1.25
HALF_NOISE = 4.4e-08
NOISE_FLOOR = FF // 16 * 3.0e-16 * (1 + 64 * (SUM_SCALE / PART_SCALE) ** 2)
NOISE_LIMIT = 1.6e-07

highest = lax.Precision.HIGHEST
feedback_rate = 0.05


def invert_low(gram_ref, out_ref, work_ref):
    rows = lax.broadcasted_iota(jnp.int32, (RANK, RANK), 0)
    lanes = lax.broadcasted_iota(jnp.int32, (RANK, RANK), 1)
    work_ref[:, :RANK] = gram_ref[...]
    work_ref[:, RANK:] = jnp.where(rows == lanes, 1.0, 0.0).astype(jnp.float32)
    own = lax.broadcasted_iota(jnp.int32, (PANEL, RANK), 0)
    for first in range(0, RANK, PANEL):
        last = first + PANEL
        panel = work_ref[first:last, :RANK]
        extra = work_ref[first:last, RANK:]
        cols = [jnp.broadcast_to(panel[:, first + t : first + t + 1], (PANEL, RANK)) for t in range(PANEL)]
        pivots = jnp.ones((PANEL, RANK), jnp.float32)
        for t in range(PANEL):
            pivot = jnp.broadcast_to(cols[t][t : t + 1], (PANEL, RANK))
            pivots = jnp.where(own == t, pivot, pivots)
            if t + 1 < PANEL:
                factor = jnp.where(own > t, cols[t] / pivot, 0.0)
                panel = panel - factor * panel[t : t + 1]
                extra = extra - factor * extra[t : t + 1]
                for u in range(t + 1, PANEL):
                    cols[u] = cols[u] - factor * cols[u][t : t + 1]
        out_ref[first:last] = extra * lax.rsqrt(pivots)
        if last < RANK:
            both = jnp.concatenate([panel, extra], axis=1)
            taken = lax.dot_general(
                panel / pivots,
                both,
                (((0,), (0,)), ((), ())),
                precision=highest,
                preferred_element_type=jnp.float32,
            )
            work_ref[last:] = work_ref[last:] - taken[last:]


def inverse_cholesky(gram_matrix):
    return pl.pallas_call(
        invert_low,
        out_shape=pltpu.VMEM((RANK, RANK), jnp.float32),
        scratch_shapes=[pltpu.VMEM((RANK, 2 * RANK), jnp.float32)],
        name="invert_low",
    )(gram_matrix)


def exchange(blocks, axis):
    return lax.all_to_all(blocks, axis, 0, 0, tiled=False)


def gather_blocks(block, axis, size):
    return exchange(jnp.broadcast_to(block[None], (size, *block.shape)), axis)


def sum_over_dp(core, part):
    rows = part.shape[0] // 2
    kept = lax.dynamic_slice_in_dim(part, core * rows, rows, 0)
    given = lax.dynamic_slice_in_dim(part, (1 - core) * rows, rows, 0)
    half = kept + lax.ppermute(given, "c", [(0, 1), (1, 0)])
    half = jnp.sum(gather_blocks(half, "x", SIDE), axis=0)
    other = lax.ppermute(half, "c", [(0, 1), (1, 0)])
    low = jnp.where(core == 0, half, other)
    high = jnp.where(core == 0, other, half)
    return jnp.concatenate([low, high], axis=0)


def to_half(rows, gram_rows, row_scale, gram_scale):
    gram_rows = gram_rows * gram_scale
    high = lax.reduce_precision(gram_rows, 5, 10)
    low = (gram_rows - high) * 2048.0
    return jnp.concatenate([(v).astype(jnp.float16) for v in (rows * row_scale, high, low)], axis=1)


def gram_of(packed, gram_scale):
    high = packed[:, SHARE : SHARE + 2].astype(jnp.float32)
    low = packed[:, SHARE + 2 :].astype(jnp.float32)
    return (high + low * (1.0 / 2048.0)) * (1.0 / gram_scale)


def outputs(blended, orthonormal, power_right, share, norm):
    momentum_out = blended - feedback_rate * jnp.dot(orthonormal, power_right.T, precision=highest)
    scale_factor = math.sqrt(D * FF / RANK)
    update = jnp.dot(orthonormal * (norm * scale_factor), power_right.T, precision=highest).astype(jnp.bfloat16)
    return (momentum_out, (share * norm).astype(jnp.bfloat16), update)


def scales(column_sums):
    return lax.rsqrt(column_sums + 1e-06)


def full_precision(blended, power_left, raw_part, gram_part):
    count = SIDE * SIDE
    slots = jnp.concatenate([raw_part.reshape(count, SHARE, RANK), gram_part.reshape(count, 2, RANK)], axis=1)
    slot = jnp.sum(exchange(slots, ("z", "y")), axis=0)
    slots = gather_blocks(slot, ("z", "y"), count)
    inverse_low = inverse_cholesky(slots[:, SHARE:].reshape(RANK, RANK))
    orthonormal = jnp.dot(power_left, inverse_low.T, precision=highest)
    power_right = jnp.dot(slots[:, :SHARE].reshape(count * SHARE, RANK), inverse_low.T, precision=highest)
    sums = jnp.sum(power_right * power_right, axis=0, keepdims=True)
    norm = scales(jnp.sum(gather_blocks(sums, ("x", "c"), 2 * SIDE), axis=(0, 1)))
    share = jnp.dot(slot[:SHARE], inverse_low.T, precision=highest)
    return outputs(blended, orthonormal, power_right, share, norm)


def local(momentum, gradient, factor_q):
    cols_local = momentum.shape[1]
    count = SIDE * SIDE
    q_cols, core = lax.optimization_barrier((jnp.broadcast_to(factor_q[None], (count, SHARE, RANK)), lax.axis_index("c")))
    q_cols = exchange(q_cols, ("z", "y"))
    q_cols, momentum, gradient, core = lax.optimization_barrier((q_cols, momentum, gradient, core))
    q_cols = q_cols.reshape(cols_local, RANK)
    blended = momentum + gradient.astype(jnp.float32)
    power_left = sum_over_dp(core, jnp.dot(blended, q_cols.astype(jnp.float32), precision=highest))
    gram_part = jnp.dot(power_left.T, power_left, precision=highest)
    raw_part = jnp.dot(blended.T, power_left, precision=highest)
    packed = to_half(raw_part.reshape(count, SHARE, RANK), gram_part.reshape(count, 2, RANK), PART_SCALE, GRAM_PART_SCALE)
    packed = exchange(packed, ("z", "y"))
    rows = packed[:, :SHARE].astype(jnp.float32)
    total = jnp.sum(rows, axis=0)
    energy = jnp.stack([jnp.sum(rows * rows, axis=(0, 1)), SPREAD * jnp.sum(total * total, axis=0)])
    energy = jnp.dot(energy, jnp.ones((RANK, RANK), jnp.float32), precision=highest)
    slot = jnp.where(energy[:1] > energy[1:], jnp.inf, total * (1.0 / PART_SCALE))
    gram_slot = jnp.sum(gram_of(packed, GRAM_PART_SCALE), axis=0)
    packed = gather_blocks(to_half(slot[None], gram_slot[None], SUM_SCALE, GRAM_SUM_SCALE)[0], ("z", "y"), count)
    rows = lax.optimization_barrier(packed[:, :SHARE].reshape(cols_local, RANK)).astype(jnp.float32)
    gram_rows = gram_of(packed, GRAM_SUM_SCALE)
    gram_matrix = gram_rows.reshape(RANK, RANK)
    inverse_low = inverse_cholesky(gram_matrix)
    orthonormal = jnp.dot(power_left, inverse_low.T, precision=highest)
    power_right = jnp.dot(rows, inverse_low.T * (1.0 / SUM_SCALE), precision=highest)
    sums = jnp.sum(power_right * power_right, axis=0)
    noise = jnp.sum(rows * rows, axis=0) * (HALF_NOISE * (1.0 + SPREAD)) + NOISE_FLOOR
    noise = jnp.sum(inverse_low * inverse_low * noise, axis=1) * (1.0 / SUM_SCALE**2)
    both = jnp.sum(gather_blocks(jnp.stack([sums, noise]), ("x", "c"), 2 * SIDE), axis=0)
    norm = scales(both[0])
    diagonal = jnp.max(jnp.where(jnp.eye(RANK, dtype=bool), gram_matrix, 0.0), axis=1)
    fine = (jnp.mean(both[1] / both[0]) < NOISE_LIMIT) & (jnp.min(diagonal) > GRAM_FLOOR)
    share = jnp.dot(slot, inverse_low.T, precision=highest)
    return lax.cond(
        fine,
        lambda: outputs(blended, orthonormal, power_right, share, norm),
        lambda: full_precision(blended, power_left, raw_part, gram_part),
    )


def solution(mesh):
    grid = Mesh(mesh.devices.reshape(SIDE, SIDE, SIDE, 2), ("z", "y", "x", "c"))
    mp, dp = ("z", "y"), ("x", "c")
    return jax.shard_map(
        local,
        mesh=grid,
        in_specs=(P(mp, dp), P(mp, dp), P((*dp, *mp), None)),
        out_specs=(P(mp, dp), P((*dp, *mp), None), P(mp, dp)),
        check_vma=False,
    )
```

```python
import math

import jax
import jax.numpy as jnp
from jax import lax
from jax.experimental import pallas as pl
from jax.experimental.pallas import tpu as pltpu
from jax.sharding import Mesh
from jax.sharding import PartitionSpec as P

D = 8192
FF = 28672
RANK = 128
SIDE = 8
SHARE = 28
PANEL = 16
PART_SCALE = 2.0**-4
SUM_SCALE = 2.0**-7
GRAM_PART_SCALE = 2.0**-8
GRAM_SUM_SCALE = 2.0**-11
GRAM_FLOOR = 0.125
SPREAD = 1.25
HALF_NOISE = 4.4e-08
NOISE_FLOOR = FF // 16 * 3.0e-16 * (1 + 64 * (SUM_SCALE / PART_SCALE) ** 2)
NOISE_LIMIT = 1.6e-07

highest = lax.Precision.HIGHEST
high = lax.Precision.HIGH
feedback_rate = 0.05


def invert_low(gram_ref, out_ref, work_ref):
    rows = lax.broadcasted_iota(jnp.int32, (RANK, RANK), 0)
    lanes = lax.broadcasted_iota(jnp.int32, (RANK, RANK), 1)
    work_ref[:, :RANK] = gram_ref[...]
    work_ref[:, RANK:] = jnp.where(rows == lanes, 1.0, 0.0).astype(jnp.float32)
    own = lax.broadcasted_iota(jnp.int32, (PANEL, RANK), 0)
    for first in range(0, RANK, PANEL):
        last = first + PANEL
        panel = work_ref[first:last, :RANK]
        extra = work_ref[first:last, RANK:]
        cols = [jnp.broadcast_to(panel[:, first + t : first + t + 1], (PANEL, RANK)) for t in range(PANEL)]
        pivots = jnp.ones((PANEL, RANK), jnp.float32)
        for t in range(PANEL):
            pivot = jnp.broadcast_to(cols[t][t : t + 1], (PANEL, RANK))
            pivots = jnp.where(own == t, pivot, pivots)
            if t + 1 < PANEL:
                factor = jnp.where(own > t, cols[t] / pivot, 0.0)
                panel = panel - factor * panel[t : t + 1]
                extra = extra - factor * extra[t : t + 1]
                for u in range(t + 1, PANEL):
                    cols[u] = cols[u] - factor * cols[u][t : t + 1]
        out_ref[first:last] = extra * lax.rsqrt(pivots)
        if last < RANK:
            both = jnp.concatenate([panel, extra], axis=1)
            taken = lax.dot_general(
                panel / pivots,
                both,
                (((0,), (0,)), ((), ())),
                precision=highest,
                preferred_element_type=jnp.float32,
            )
            work_ref[last:] = work_ref[last:] - taken[last:]


def inverse_cholesky(gram_matrix):
    return pl.pallas_call(
        invert_low,
        out_shape=pltpu.VMEM((RANK, RANK), jnp.float32),
        scratch_shapes=[pltpu.VMEM((RANK, 2 * RANK), jnp.float32)],
        name="invert_low",
    )(gram_matrix)


def exchange(blocks, axis):
    return lax.all_to_all(blocks, axis, 0, 0, tiled=False)


def gather_blocks(block, axis, size):
    return exchange(jnp.broadcast_to(block[None], (size, *block.shape)), axis)


def sum_over_dp(core, part):
    rows = part.shape[0] // 2
    kept = lax.dynamic_slice_in_dim(part, core * rows, rows, 0)
    given = lax.dynamic_slice_in_dim(part, (1 - core) * rows, rows, 0)
    half = kept + lax.ppermute(given, "c", [(0, 1), (1, 0)])
    half = jnp.sum(gather_blocks(half, "x", SIDE), axis=0)
    other = lax.ppermute(half, "c", [(0, 1), (1, 0)])
    low = jnp.where(core == 0, half, other)
    high = jnp.where(core == 0, other, half)
    return jnp.concatenate([low, high], axis=0)


def to_half(rows, gram_rows, row_scale, gram_scale):
    gram_rows = gram_rows * gram_scale
    coarse = lax.reduce_precision(gram_rows, 5, 10)
    fine = (gram_rows - coarse) * 2048.0
    return jnp.concatenate([v.astype(jnp.float16) for v in (rows * row_scale, coarse, fine)], axis=1)


def gram_of(packed, gram_scale):
    high = packed[:, SHARE : SHARE + 2].astype(jnp.float32)
    low = packed[:, SHARE + 2 :].astype(jnp.float32)
    return (high + low * (1.0 / 2048.0)) * (1.0 / gram_scale)


def outputs(blended, orthonormal, power_right, share, norm):
    momentum_out = blended - feedback_rate * jnp.dot(orthonormal, power_right.T, precision=high)
    scale_factor = math.sqrt(D * FF / RANK)
    update = jnp.dot(orthonormal * (norm * scale_factor), power_right.T, precision=high).astype(jnp.bfloat16)
    return (momentum_out, (share * norm).astype(jnp.bfloat16), update)


def scales(column_sums):
    return lax.rsqrt(column_sums + 1e-06)


def full_precision(blended, power_left, gram_part):
    count = SIDE * SIDE
    raw_part = jnp.dot(blended.T, power_left, precision=highest)
    slots = jnp.concatenate([raw_part.reshape(count, SHARE, RANK), gram_part.reshape(count, 2, RANK)], axis=1)
    slot = jnp.sum(exchange(slots, ("z", "y")), axis=0)
    slots = gather_blocks(slot, ("z", "y"), count)
    inverse_low = inverse_cholesky(slots[:, SHARE:].reshape(RANK, RANK))
    orthonormal = jnp.dot(power_left, inverse_low.T, precision=highest)
    power_right = jnp.dot(slots[:, :SHARE].reshape(count * SHARE, RANK), inverse_low.T, precision=highest)
    sums = jnp.sum(power_right * power_right, axis=0, keepdims=True)
    norm = scales(jnp.sum(gather_blocks(sums, ("x", "c"), 2 * SIDE), axis=(0, 1)))
    share = jnp.dot(slot[:SHARE], inverse_low.T, precision=highest)
    return outputs(blended, orthonormal, power_right, share, norm)


def local(momentum, gradient, factor_q):
    cols_local = momentum.shape[1]
    count = SIDE * SIDE
    q_cols, core = lax.optimization_barrier((jnp.broadcast_to(factor_q[None], (count, SHARE, RANK)), lax.axis_index("c")))
    q_cols = exchange(q_cols, ("z", "y"))
    q_cols, momentum, core = lax.optimization_barrier((q_cols, momentum, core))
    q_cols = q_cols.reshape(cols_local, RANK)
    blended = momentum + gradient.astype(jnp.float32)
    power_left = sum_over_dp(core, jnp.dot(blended, q_cols.astype(jnp.float32), precision=highest))
    gram_part = jnp.dot(power_left.T, power_left, precision=highest)
    raw_part = jnp.dot(blended.T, power_left, precision=high)
    packed = to_half(raw_part.reshape(count, SHARE, RANK), gram_part.reshape(count, 2, RANK), PART_SCALE, GRAM_PART_SCALE)
    packed = exchange(packed, ("z", "y"))
    rows = packed[:, :SHARE].astype(jnp.float32)
    total = jnp.sum(rows, axis=0)
    energy = jnp.stack([jnp.sum(rows * rows, axis=(0, 1)), SPREAD * jnp.sum(total * total, axis=0)])
    energy = jnp.dot(energy, jnp.ones((RANK, RANK), jnp.float32), precision=highest)
    slot = jnp.where(energy[:1] > energy[1:], jnp.inf, total * (1.0 / PART_SCALE))
    gram_slot = jnp.sum(gram_of(packed, GRAM_PART_SCALE), axis=0)
    packed = gather_blocks(to_half(slot[None], gram_slot[None], SUM_SCALE, GRAM_SUM_SCALE)[0], ("z", "y"), count)
    rows = lax.optimization_barrier(packed[:, :SHARE].reshape(cols_local, RANK)).astype(jnp.float32)
    gram_rows = gram_of(packed, GRAM_SUM_SCALE)
    gram_matrix = gram_rows.reshape(RANK, RANK)
    inverse_low = inverse_cholesky(gram_matrix)
    orthonormal = jnp.dot(power_left, inverse_low.T, precision=highest)
    power_right = jnp.dot(rows, inverse_low.T * (1.0 / SUM_SCALE), precision=high)
    sums = jnp.sum(power_right * power_right, axis=0)
    noise = jnp.sum(rows * rows, axis=0) * (HALF_NOISE * (1.0 + SPREAD)) + NOISE_FLOOR
    noise = jnp.sum(inverse_low * inverse_low * noise, axis=1) * (1.0 / SUM_SCALE**2)
    both = jnp.sum(gather_blocks(jnp.stack([sums, noise]), ("x", "c"), 2 * SIDE), axis=0)
    norm = scales(both[0])
    diagonal = jnp.max(jnp.where(jnp.eye(RANK, dtype=bool), gram_matrix, 0.0), axis=1)
    fine = (jnp.mean(both[1] / both[0]) < NOISE_LIMIT) & (jnp.min(diagonal) > GRAM_FLOOR)
    share = jnp.dot(slot, inverse_low.T, precision=highest)
    return lax.cond(
        fine,
        lambda: outputs(blended, orthonormal, power_right, share, norm),
        lambda: full_precision(blended, power_left, gram_part),
    )


def solution(mesh):
    grid = Mesh(mesh.devices.reshape(SIDE, SIDE, SIDE, 2), ("z", "y", "x", "c"))
    mp, dp = ("z", "y"), ("x", "c")
    return jax.shard_map(
        local,
        mesh=grid,
        in_specs=(P(mp, dp), P(mp, dp), P((*dp, *mp), None)),
        out_specs=(P(mp, dp), P((*dp, *mp), None), P(mp, dp)),
        check_vma=False,
    )
```
